512 devices in a mesh: seq: 64 (over y_lo, z, core), dp: 8 (over y_hi, x).
Axes of the slice: x: 4, y: 4 (y_hi: 2, y_lo: 2; y = y_hi * 2 + y_lo), z: 16, core: 2. Of those that a mesh axis runs over, the one named last changes fastest.
Arguments:
- features: float32 [8, 16384, 512], P('dp', 'seq'), may hold values from -64 to 64
- norm_gain: float32 [2, 512], replicated, may hold values from 0.25 to 1.75
- filters: float32 [4, 512], replicated, may hold values from -1 to 1
- level_weights: float32 [15, 512], replicated, may hold values from -1.2 to 1.2
- glu_weight: float32 [512, 1024], P('dp'), may hold values from -0.25 to 0.25
- expand_weight: float32 [512, 2048], P('dp'), may hold values from -0.25 to 0.25
- reduce_weight: float32 [2048, 512], P('dp'), may hold values from -0.125 to 0.125
Outputs:
- layer_out: float32 [8, 16384, 512], P('dp', 'seq')
The draws below stay inside these ranges and needn't reach their ends.
All inputs are finite; a program needn't handle non-finite values.
Results may differ from the reference program's by a relative error of at most 0.000069.
Values sent between devices are 32-bit elements; how exact they have to be, the bound alone decides.
No kernel may reach another device: no remote copies, remote signals or barrier semaphores. Data moves between devices by JAX's collectives and lax.ppermute only.
A program may use at most 64 MiB of HBM per device.

```python
import math
import jax
import jax.numpy as jnp
from jax import lax

D = 512
FF = 2048
LEVELS = 14
SEQ = 16384
BATCH = 8


def draw_features(key, part):
    key_base, key_rows, key_cols = jax.random.split(key, 3)
    base = jax.random.truncated_normal(key_base, -4.0, 4.0, (BATCH, SEQ, D), jnp.float32)
    row_scale = jnp.exp(jax.random.uniform(key_rows, (BATCH, SEQ, 1), jnp.float32, math.log(0.4), math.log(4.0)))
    col_scale = jnp.exp(jax.random.uniform(key_cols, (D,), jnp.float32, math.log(0.4), math.log(4.0)))
    return base * row_scale * col_scale


def draw_filters(key, part):
    angles = jax.random.uniform(key, (2, D), jnp.float32, -math.pi, math.pi)
    return jnp.stack([jnp.cos(angles[0]), jnp.sin(angles[0]), jnp.cos(angles[1]), jnp.sin(angles[1])], axis=0)


def block_levels(key, dims, cuts, least, largest):
    level, own = 1.0, jax.random.fold_in(key, 6)
    for position, parts in cuts:
        heights = jnp.exp(jax.random.uniform(jax.random.fold_in(own, position), (parts,), jnp.float32, least / len(cuts), largest / len(cuts)))
        level = level * jnp.repeat(heights, dims[position] // parts).reshape([-1 if axis == position else 1 for axis in range(len(dims))])
    return level


def scatter_about(stream_key, dims, deviation, most, shards=(), dtype=jnp.bfloat16):
    gain = block_levels(stream_key, dims, shards, -0.22, 0.18) if shards else 1.0
    result = jax.random.normal(stream_key, dims, jnp.float32) * deviation * gain
    return jnp.minimum(jnp.maximum(result, -most), most).astype(dtype)


def setup_inputs(seed: int = 0) -> dict:
    streams_of = jax.random.split(jax.random.key(seed), 8)
    features = draw_features(jax.random.fold_in(streams_of[7], 71), 0)
    norm_gain = jnp.clip(1.0 + 0.15 * jax.random.normal(streams_of[1], (2, D), jnp.float32), 0.25, 1.75)
    filters = draw_filters(jax.random.fold_in(streams_of[7], 71), 0)
    level_weights = scatter_about(streams_of[3], (LEVELS + 1, D), 0.3, 1.2, (), jnp.float32)
    glu_weight = scatter_about(streams_of[4], (D, 2 * D), D ** -0.5, 0.25, ((0, 8),), jnp.float32)
    expand_weight = scatter_about(streams_of[5], (D, FF), D ** -0.5, 0.25, ((0, 8),), jnp.float32)
    reduce_weight = scatter_about(streams_of[6], (FF, D), FF ** -0.5, 0.125, ((0, 8),), jnp.float32)
    return dict(features=features, norm_gain=norm_gain, filters=filters, level_weights=level_weights, glu_weight=glu_weight, expand_weight=expand_weight, reduce_weight=reduce_weight)


def layer_norm(values, gain_row):
    average = lax.optimization_barrier(jnp.mean(values, axis=-1, keepdims=True))
    centred = values - average
    variance = lax.optimization_barrier(jnp.mean(centred * centred, axis=-1, keepdims=True))
    return centred * lax.rsqrt(variance + 1e-05) * gain_row

def reference(features, norm_gain, filters, level_weights, glu_weight, expand_weight, reduce_weight):

    def mix_sequence(sequence):
        normed = layer_norm(sequence, norm_gain[0])
        current = normed
        detail_sum = jnp.zeros_like(normed)
        for level_step in range(LEVELS):
            spacing = 2 ** level_step
            earlier = jnp.concatenate([jnp.zeros((spacing, D), jnp.float32), current[:SEQ - spacing]], axis=0)
            detail_sum = detail_sum + level_weights[level_step] * (filters[2] * earlier + filters[3] * current)
            current = filters[0] * earlier + filters[1] * current
        detail_sum = detail_sum + level_weights[LEVELS] * current
        activated = jax.nn.gelu(detail_sum, approximate=False)
        projected = jnp.dot(activated, glu_weight, precision=lax.Precision.HIGHEST, preferred_element_type=jnp.float32)
        residual = sequence + projected[:, :D] * jax.nn.sigmoid(projected[:, D:])
        second = layer_norm(residual, norm_gain[1])
        hidden = jax.nn.relu(jnp.dot(second, expand_weight, precision=lax.Precision.HIGHEST, preferred_element_type=jnp.float32))
        return residual + jnp.dot(hidden, reduce_weight, precision=lax.Precision.HIGHEST, preferred_element_type=jnp.float32)
    return lax.map(mix_sequence, features)
```

```python
import jax
import jax.numpy as jnp
from jax import lax
from jax.experimental import pallas as pl
from jax.experimental.pallas import tpu as pltpu
from jax.sharding import Mesh
from jax.sharding import PartitionSpec as P

SEQ_AXES = ("ylo", "z", "core")
LANES = 128
ROWS = 8


def norm_rows(values, gain_row):
    average = jnp.mean(values, axis=-1, keepdims=True)
    centred = values - average
    variance = jnp.mean(centred * centred, axis=-1, keepdims=True)
    return centred * lax.rsqrt(variance + 1e-05) * gain_row


def norm_turn_kernel(x_ref, gain_ref, out_ref):
    normed = norm_rows(x_ref[...], gain_ref[0:1, :])
    turned = normed.T
    groups, halves = out_ref.shape[0], out_ref.shape[1]
    for half in range(halves):
        out_ref[:, half] = turned[:, half * LANES : (half + 1) * LANES].reshape(groups, ROWS, LANES)


def norm_turn(x, gains):
    extent, channels = x.shape
    return pl.pallas_call(
        norm_turn_kernel,
        out_shape=jax.ShapeDtypeStruct((channels // ROWS, extent // LANES, ROWS, LANES), jnp.float32),
        name="norm_turn",
    )(x, gains)


def levels_kernel(levels, x_ref, coef_ref, out_ref, level_ref):
    tiles = x_ref.shape[0]
    pad = tiles // 2
    chunk = 16
    table = coef_ref[...]

    def coef(index):
        return jnp.broadcast_to(table[:, index : index + 1], (ROWS, LANES))[None]

    low_lag, low_now, high_lag, high_now = (coef(index) for index in range(4))
    level_ref[0:pad] = jnp.zeros((pad, ROWS, LANES), jnp.float32)
    level_ref[pad:] = x_ref[...]
    lane = lax.broadcasted_iota(jnp.int32, (chunk, ROWS, LANES), 2)
    for step in range(levels):
        weight = coef(4 + step)

        def visit(index, carry, step=step, weight=weight):
            start = tiles - (index + 1) * chunk
            now = level_ref[pl.ds(pad + start, chunk)]
            if 2**step < LANES:
                before = level_ref[pl.ds(pad + start - 1, chunk)]
                earlier = pltpu.roll(jnp.where(lane >= LANES - 2**step, before, now), 2**step, 2)
            else:
                earlier = level_ref[pl.ds(pad + start - 2**step // LANES, chunk)]
            detail = weight * (high_lag * earlier + high_now * now)
            later = low_lag * earlier + low_now * now
            level_ref[pl.ds(pad + start, chunk)] = later
            if step:
                detail = out_ref[pl.ds(start, chunk)] + detail
            if step == levels - 1:
                detail = detail + coef(4 + levels) * later
            out_ref[pl.ds(start, chunk)] = detail
            return carry

        lax.fori_loop(0, tiles // chunk, visit, 0)


def all_levels(x, table, levels):
    tiles = x.shape[0]
    return pl.pallas_call(
        lambda *refs: levels_kernel(levels, *refs),
        out_shape=jax.ShapeDtypeStruct(x.shape, jnp.float32),
        scratch_shapes=[pltpu.VMEM((tiles + tiles // 2, ROWS, LANES), jnp.float32)],
        name="all_levels",
    )(x, table)


def product(operand, weights):
    return jnp.dot(operand, weights, precision=lax.Precision.HIGH, preferred_element_type=jnp.float32)


def body(features, norm_gain, filters, level_weights, glu_weight, expand_weight, reduce_weight):
    batches, extent, channels = features.shape
    levels = level_weights.shape[0] - 1
    shards = lax.axis_size("dp")
    hidden_units = expand_weight.shape[1]
    core = lax.axis_index("core")
    places = lax.axis_size("ylo") * lax.axis_size("z") * lax.axis_size("core")
    half = channels // 2
    depth = glu_weight.shape[0]
    rows = features.reshape(extent, channels)

    def mine(array, first):
        return jnp.where(core == 0, first(array, 0), first(array, 1))

    glu_half = mine(
        glu_weight.reshape(depth, 2, 2, half), lambda a, c: a[:, :, c].reshape(depth, channels)
    )
    group = hidden_units // shards
    expand_half = mine(
        expand_weight.reshape(depth, shards, 2, group // 2),
        lambda a, c: a[:, :, c].reshape(depth, hidden_units // 2),
    )
    reduce_half = mine(reduce_weight, lambda a, c: a[c * (group // 2) : (c + 1) * (group // 2)])
    packed = jnp.concatenate(
        [glu_half, expand_half[:, :channels], expand_half[:, channels:], reduce_half], axis=0
    )
    own = lax.all_gather(packed, "dp", axis=0)

    turned = norm_turn(rows, norm_gain)
    spread = lax.all_to_all(turned, SEQ_AXES, 0, 0, tiled=True)
    place = lax.axis_index(SEQ_AXES)
    table = jnp.concatenate([filters, level_weights], axis=0)
    table = lax.dynamic_slice(table, (0, place * ROWS), (table.shape[0], ROWS)).T
    mixed = all_levels(spread.reshape(-1, ROWS, LANES), table, levels)
    back = lax.all_to_all(mixed.reshape(turned.shape), SEQ_AXES, 0, 0, tiled=True)
    back = jnp.transpose(back, (1, 3, 0, 2)).reshape(extent, channels)

    activated = jax.nn.gelu(back, approximate=False)
    swap = [(0, 1), (1, 0)]
    other_glu = lax.ppermute(own[:, :depth], "core", swap)
    other_rest = lax.ppermute(own[:, depth:], "core", swap)

    def gated(block):
        projected = product(activated, block.reshape(channels, channels))
        return projected[:, :half] * jax.nn.sigmoid(projected[:, half:])

    own_gated, other_gated = gated(own[:, :depth]), gated(other_glu)
    mixture = jnp.where(
        core == 0,
        jnp.concatenate([own_gated, other_gated], axis=1),
        jnp.concatenate([other_gated, own_gated], axis=1),
    )
    residual = rows + mixture
    second = norm_rows(residual, norm_gain[1])
    total = residual
    for rest in (own[:, depth:], other_rest):
        first = product(second, rest[:, :depth].reshape(channels, channels))
        last = product(second, rest[:, depth : 2 * depth].reshape(channels, channels))
        hidden = jax.nn.relu(jnp.concatenate([first, last], axis=1))
        total = total + product(hidden, rest[:, 2 * depth :].reshape(hidden_units // 2, channels))
    return total.reshape(batches, extent, channels)


def solution(mesh):
    dp = mesh.shape["dp"]
    depth = mesh.shape["seq"] // 4
    split = Mesh(mesh.devices.reshape(2, depth, 2, dp), SEQ_AXES + ("dp",))
    data = P("dp", SEQ_AXES, None)
    return jax.shard_map(
        body,
        mesh=split,
        in_specs=(data, P(), P(), P(), P("dp", None), P("dp", None), P("dp", None)),
        out_specs=data,
        check_vma=False,
    )
```
